1024 devices in a mesh: dp: 16 (over y, core), section: 4 (over x), ctx: 16 (over z).
Axes of the slice: x: 4, y: 8, z: 16, core: 2. Of those that a mesh axis runs over, the one named last changes fastest.
Arguments:
- queries: bfloat16 [4, 16, 2048, 4096], P('section', 'dp', 'ctx'), may hold values from -30 to 30
- keys_values: bfloat16 [4, 16, 2048, 1024], P('section', 'dp', 'ctx'), may hold values from -30 to 30
- random_blocks: int32 [16, 16, 4, 4], P('dp'), may hold values from 0 to 15, as said below
- global_blocks: int32 [16, 2], P('dp'), may hold values from 0 to 15
- doc_lengths: int32 [16, 4], P('dp'), may hold values from 1 to 1024, 2048 in all within a row
- cotangent: bfloat16 [4, 16, 2048, 4096], P('section', 'dp', 'ctx'), may hold values from -1.5 to 1.5
Outputs:
- stream: bfloat16 [4, 16, 2048, 4096], P('section', 'dp', 'ctx')
- gain_grad: float32 [4, 4096], P('section')
The draws below stay inside these ranges and needn't reach their ends.
Inputs may be any that keep to these rules, and one draw needn't show every extreme that they name: `random_blocks`: for each query block, its 4 x 4 entries over all key heads name every block of the sequence exactly 1 times.
All inputs are finite; a program needn't handle non-finite values.
Results may differ from the reference program's by a relative error of at most 0.0062.
Values may be sent and summed in bfloat16 or wider, within the bound.
A program may use at most 32 MiB of HBM per device.

```python
import math
import jax
import jax.numpy as jnp
import numpy as np
from jax import lax

HEADS = 32
KVH = 4
HD = 128
BLOCK = 128
RAND = 4
GLOBALS = 2
DOCS = 4
GROUP = 8
NBLK = 16
LEN = 2048
SEQS = 16
SECTIONS = 4
DOC_MOST = 1024


def draw_pair(key):
    base_key = jax.random.fold_in(key, 11)
    key_query, key_keys, key_values = jax.random.split(base_key, 3)
    query_shape = (SECTIONS, SEQS, LEN, KVH, GROUP, HD)
    head_shape = (SECTIONS, SEQS, LEN, KVH, HD)
    query_vals = jax.random.normal(key_query, query_shape, jnp.float32)
    key_vals = jax.random.normal(key_keys, head_shape, jnp.float32)
    value_vals = 2.0 * jax.random.normal(key_values, head_shape, jnp.float32)
    query_flat = query_vals.reshape(SECTIONS, SEQS, LEN, KVH * GROUP * HD)
    pair_flat = jnp.concatenate([key_vals.reshape(SECTIONS, SEQS, LEN, KVH * HD), value_vals.reshape(SECTIONS, SEQS, LEN, KVH * HD)], axis=-1)
    return (query_flat, pair_flat)


def draw_queries(key, part):
    return draw_pair(key)[0].astype(jnp.bfloat16)


def draw_keys_values(key, part):
    return draw_pair(key)[1].astype(jnp.bfloat16)


def draw_random_blocks(key, part):
    item_count = KVH * RAND
    key_list = jax.random.split(jax.random.fold_in(key, 23), SEQS * NBLK)
    orders = jax.vmap(lambda one_key: jax.random.permutation(one_key, item_count))(key_list)
    return (orders % NBLK).reshape(SEQS, NBLK, KVH, RAND).astype(jnp.int32)


def touch_ends(array, rng, low, high):
    place = [jax.random.randint(jax.random.fold_in(rng, axis), (), 0, length) for axis, length in enumerate(array.shape)]
    longest = array.shape.index(max(array.shape))
    beside = place[:longest] + [(place[longest] + 1) % array.shape[longest]] + place[longest + 1:]
    return array.at[tuple(place)].set(low).at[tuple(beside)].set(high)


def levels(own_key, extent, cuts, least, top_value):
    level, own = 1.0, jax.random.fold_in(own_key, 6)
    for dim, blocks in cuts:
        steps = jnp.exp(jax.random.uniform(jax.random.fold_in(own, dim), (blocks,), jnp.float32, least / len(cuts), top_value / len(cuts)))
        level = level * jnp.repeat(steps, extent[dim] // blocks).reshape([-1 if axis == dim else 1 for axis in range(len(extent))])
    return level


def length_profile(count, total, most, skew):
    loads = [(1 << 20) // math.isqrt(rank ** skew) + 1 for rank in range(2, count + 1)]
    surplus, given = total - most - (count - 1), [1] * (count - 1)
    while surplus > 0:
        movable = [i for i in range(count - 1) if given[i] < most]
        mass, remaining = sum([loads[i] for i in movable]), surplus
        for i in movable:
            addition = min(most - given[i], max(1, remaining * loads[i] // mass), surplus)
            given[i] = given[i] + addition
            surplus = surplus - addition
    return np.array([most] + given)


def ragged(own_key, number_of, total, limit, slope):
    if number_of == 2:
        one = jax.random.randint(own_key, (), max(1, total - limit), min(limit, total - 1) + 1)
        return jnp.stack([one, total - one])
    lengths = jnp.asarray(length_profile(number_of, total, limit, slope), jnp.int32)
    twos = (number_of - 1) // 2
    donor, taker = lengths[1:1 + 2 * twos:2], lengths[2:2 + 2 * twos:2]
    slack = jnp.minimum(donor - 1, limit - taker)
    shifted = jax.random.randint(jax.random.fold_in(own_key, 1), (twos,), 0, 1 << 20) % (slack + 1)
    lengths = lengths.at[1:1 + 2 * twos:2].set(donor - shifted).at[2:2 + 2 * twos:2].set(taker + shifted)
    return lengths[jax.random.permutation(jax.random.fold_in(own_key, 2), number_of)]


def noise(stream_key, shape, width, reach, shards=(), kind=jnp.bfloat16):
    array = width * jax.random.normal(stream_key, shape, jnp.float32)
    if shards:
        array = array * levels(stream_key, shape, shards, -0.22, 0.18)
    return jnp.clip(array, -reach, reach).astype(kind)


def setup_inputs(seed: int = 0) -> dict:
    arg_keys = jax.random.split(jax.random.key(seed), 7)
    queries = draw_queries(jax.random.fold_in(arg_keys[6], 71), 0)
    keys_values = draw_keys_values(jax.random.fold_in(arg_keys[6], 71), 0)
    random_blocks = draw_random_blocks(jax.random.fold_in(arg_keys[6], 71), 0)
    global_blocks = touch_ends(jax.random.randint(arg_keys[3], (SEQS, GLOBALS), 0, NBLK), jax.random.fold_in(arg_keys[3], 1), 0, NBLK - 1).astype(jnp.int32)
    doc_lengths = jax.vmap(lambda own: ragged(own, DOCS, LEN, DOC_MOST, 2))(jax.random.split(arg_keys[4], SEQS)).reshape((SEQS, DOCS)).astype(jnp.int32)
    cotangent = noise(arg_keys[5], (SECTIONS, SEQS, LEN, HEADS * HD), 0.25, 1.5, ((0, 4), (1, 16), (2, 16)))
    return {"queries": queries, "keys_values": keys_values, "random_blocks": random_blocks, "global_blocks": global_blocks, "doc_lengths": doc_lengths, "cotangent": cotangent}


def doc_index(doc_ends, positions):
    return lax.optimization_barrier(jnp.sum((doc_ends <= positions[..., None]).astype(jnp.int32), axis=-1))

def attend_block(query_rows, key_rows, value_rows, allowed):
    scores = jnp.einsum('qhgd,hkd->hgqk', query_rows, key_rows) / math.sqrt(HD)
    scores = jnp.where(allowed[:, None], scores, -1e+30)
    row_max = lax.optimization_barrier(jnp.max(scores, axis=-1, keepdims=True))
    weights = jnp.where(allowed[:, None], jnp.exp(scores - row_max), 0.0)
    weight_sum = lax.optimization_barrier(jnp.sum(weights, axis=-1))
    rounded = lax.optimization_barrier(weights.astype(jnp.bfloat16)).astype(jnp.float32)
    product = jnp.einsum('hgqk,hkd->qhgd', rounded, value_rows)
    return product / jnp.transpose(weight_sum, (2, 0, 1))[..., None]

def section_attention(query_seq, kv_seq, block_lists, global_ids, doc_ends):
    padded = jnp.pad(kv_seq, ((BLOCK, BLOCK), (0, 0)))
    blocked = kv_seq.reshape(NBLK, BLOCK, 2, KVH, HD)
    row_steps = jnp.arange(BLOCK, dtype=jnp.int32)
    global_rows = jnp.concatenate([lax.dynamic_slice_in_dim(kv_seq, (global_ids[global_slot] * BLOCK).astype(jnp.int32), BLOCK, 0) for global_slot in range(GLOBALS)], axis=0)
    global_pos = (global_ids[:, None] * BLOCK + row_steps[None, :]).reshape(-1).astype(jnp.int32)
    head_index = jnp.arange(KVH, dtype=jnp.int32)

    def one_block(block_id):
        first_row = (block_id * BLOCK).astype(jnp.int32)
        query_rows = lax.dynamic_slice_in_dim(query_seq, first_row, BLOCK, 0).astype(jnp.float32)
        query_rows = query_rows.reshape(BLOCK, KVH, GROUP, HD)
        window_rows = lax.dynamic_slice_in_dim(padded, first_row, 3 * BLOCK, 0)
        window_pos = first_row - BLOCK + jnp.arange(3 * BLOCK, dtype=jnp.int32)
        shared_rows = jnp.concatenate([window_rows, global_rows], axis=0)
        shared_pos = jnp.concatenate([window_pos, global_pos])
        shared_heads = jnp.transpose(shared_rows.reshape(-1, 2, KVH, HD), (2, 0, 1, 3))
        own_lists = block_lists[block_id]
        random_heads = blocked[own_lists, :, :, head_index[:, None]].reshape(KVH, RAND * BLOCK, 2, HD)
        all_heads = jnp.concatenate([jnp.broadcast_to(shared_heads, (KVH,) + shared_heads.shape[1:]), random_heads], axis=1).astype(jnp.float32)
        random_pos = (own_lists[:, :, None] * BLOCK + row_steps).reshape(KVH, -1).astype(jnp.int32)
        query_doc = doc_index(doc_ends, first_row + row_steps)
        shared_ok = (shared_pos >= 0) & (shared_pos < LEN)
        shared_ok = shared_ok[None, :] & (doc_index(doc_ends, shared_pos)[None, :] == query_doc[:, None])
        random_ok = doc_index(doc_ends, random_pos)[:, None, :] == query_doc[None, :, None]
        allowed = jnp.concatenate([jnp.broadcast_to(shared_ok, (KVH,) + shared_ok.shape), random_ok], axis=2)
        result = attend_block(query_rows, all_heads[:, :, 0], all_heads[:, :, 1], allowed)
        return result.reshape(BLOCK, HEADS * HD)
    outputs = lax.map(one_block, jnp.arange(NBLK, dtype=jnp.int32))
    return outputs.reshape(LEN, HEADS * HD)

def reference(queries, keys_values, random_blocks, global_blocks, doc_lengths, cotangent):

    def one_sequence(seq_id):
        doc_ends = jnp.cumsum(doc_lengths[seq_id]).astype(jnp.int32)
        previous = jnp.zeros((LEN, HEADS * HD), jnp.float32)
        streams = []
        gradient_terms = []
        for section_id in range(SECTIONS):
            attention = section_attention(queries[section_id, seq_id], keys_values[section_id, seq_id], random_blocks[seq_id], global_blocks[seq_id], doc_ends)
            attention = lax.optimization_barrier(attention.astype(jnp.bfloat16)).astype(jnp.float32)
            if section_id == 0:
                handed = attention.astype(jnp.bfloat16)
            else:
                handed = (previous + attention).astype(jnp.bfloat16)
            widened = handed.astype(jnp.float32)
            previous = widened
            inverse = lax.rsqrt(lax.optimization_barrier(jnp.mean(widened * widened, axis=-1, keepdims=True)) + 1e-06)
            gradient_terms.append(lax.optimization_barrier(jnp.sum(cotangent[section_id, seq_id].astype(jnp.float32) * widened * inverse, axis=0)))
            streams.append(handed)
        return (jnp.stack(streams), jnp.stack(gradient_terms))
    stream, gradient_terms = lax.map(one_sequence, jnp.arange(SEQS, dtype=jnp.int32))
    return (jnp.transpose(stream, (1, 0, 2, 3)), lax.optimization_barrier(jnp.sum(gradient_terms, axis=0)) / SEQS)
```

```python
import functools
import math

import jax
import jax.numpy as jnp
from jax import lax
from jax.experimental import pallas as pl
from jax.experimental.pallas import tpu as pltpu
from jax.sharding import PartitionSpec as P

HEADS = 32
KVH = 4
HD = 128
RAND = 4
GLOBALS = 2
GROUP = 8
DOCS = 4
BLOCK = 128
LISTED = 3 + GLOBALS + RAND
PAIRS = HEADS // 2
MESH = pl.DeviceIdType.MESH
FACTOR = math.log2(math.e) / math.sqrt(HD)
LAG = 2


def body(
    counts,
    random_ref, global_ref, length_ref, q_hbm, kv_hbm, cot_hbm,
    stream_hbm, gain_ref,
    kv0, kv1, kv2, kv3, qs, cs, stream, arrived, keys, values, onehot, squares,
    terms, scattered, crossed, gathered,
    ag_send, ag_recv, kv_sem, q_sem, c_sem, out_sem,
    relay_send, relay_recv, rs_send, rs_recv, z_send, z_recv, f_send, f_recv,
):
    dp_count, section_count, n = counts
    dp, section, me = lax.axis_index("dp"), lax.axis_index("section"), lax.axis_index("ctx")
    half = n // 2
    kvs = (kv0, kv1, kv2, kv3)
    right, left = lax.rem(me + 1, n), lax.rem(me + n - 1, n)

    def local_kv(h):
        copies = []
        for part in range(2):
            column = part * KVH * HD + h * HD
            copies.append(pltpu.make_async_copy(
                kv_hbm.at[0, 0, :, pl.ds(column, HD)],
                kvs[h].at[me, pl.ds(part * BLOCK, BLOCK)],
                kv_sem.at[h, part],
            ))
        return copies

    def q_copy(u):
        return pltpu.make_async_copy(
            q_hbm.at[0, 0, :, pl.ds(pl.multiple_of(u * HD, HD), HD)], qs.at[u], q_sem.at[u])

    def c_copy(u):
        return pltpu.make_async_copy(
            cot_hbm.at[0, 0, :, pl.ds(pl.multiple_of(u * HD, HD), HD)], cs.at[u], c_sem.at[u])

    def out_copy(u):
        return pltpu.make_async_copy(
            stream.at[u], stream_hbm.at[0, 0, :, pl.ds(pl.multiple_of(u * HD, HD), HD)], out_sem.at[u])

    def ring(h, d, t, last):
        sign = 1 if d == 0 else -1
        origin = lax.rem(me - sign * (t - 1) + 2 * n, n)
        place = kvs[h].at[origin, pl.ds(d * BLOCK, BLOCK)] if last else kvs[h].at[origin]
        return pltpu.make_async_remote_copy(
            src_ref=place, dst_ref=place,
            send_sem=ag_send.at[h, d, t - 1], recv_sem=ag_recv.at[h, d, t - 1],
            device_id={"ctx": right if d == 0 else left}, device_id_type=MESH)

    def ring_arrival(h, d, t, last):
        sign = 1 if d == 0 else -1
        origin = lax.rem(me - sign * t + 2 * n, n)
        place = kvs[h].at[origin, pl.ds(d * BLOCK, BLOCK)] if last else kvs[h].at[origin]
        return pltpu.make_async_remote_copy(
            src_ref=place, dst_ref=place,
            send_sem=ag_send.at[h, d, t - 1], recv_sem=ag_recv.at[h, d, t - 1],
            device_id={"ctx": right if d == 0 else left}, device_id_type=MESH)

    def ring_start(heads):
        for h in heads:
            for d in range(2):
                ring(h, d, 1, False).start()

    def ring_step(heads, t):
        @pl.when(t < half)
        def _():
            for h in heads:
                for d in range(2):
                    ring_arrival(h, d, t - 1, False).wait_recv()
                    ring(h, d, t, False).start()

        @pl.when(t == half)
        def _():
            for h in heads:
                for d in range(2):
                    ring_arrival(h, d, half - 1, False).wait_recv()
                    ring(h, d, half, True).start()

    def ring_finish(heads):
        for h in heads:
            for d in range(2):
                ring_arrival(h, d, half, True).wait_recv()

    barrier = pltpu.get_barrier_semaphore()
    for h in range(KVH):
        for copy in local_kv(h):
            copy.start()
    for target in (left, right):
        pl.semaphore_signal(barrier, inc=1, device_id={"ctx": target}, device_id_type=MESH)
    for step in (1, section_count - 1):
        pl.semaphore_signal(
            barrier, inc=1, device_id={"section": lax.rem(section + step, section_count)}, device_id_type=MESH)
    for step in range(1, dp_count):
        pl.semaphore_signal(
            barrier, inc=1, device_id={"dp": lax.rem(dp + step, dp_count)}, device_id_type=MESH)

    def start_inputs(u, carry):
        q_copy(u).start()
        c_copy(u).start()
        return carry

    lax.fori_loop(0, HEADS, start_inputs, 0)
    pl.semaphore_wait(barrier, 4 + dp_count - 1)
    for h in range(KVH):
        for copy in local_kv(h):
            copy.wait()
    ring_start((0, 1))

    ends = []
    total = 0
    for d in range(DOCS):
        total = total + length_ref[0, d]
        ends.append(total)
    lanes = lax.broadcasted_iota(jnp.int32, (BLOCK, HD), 1)
    rows = lax.broadcasted_iota(jnp.int32, (BLOCK, HD), 0)

    def doc_of(block):
        position = rows + block * BLOCK
        doc = jnp.zeros((BLOCK, HD), jnp.int32)
        for end in ends:
            doc = doc + jnp.where(position >= end, 1, 0)
        return doc

    own_hot = jnp.where(doc_of(me) == lanes, 1.0, 0.0).astype(jnp.bfloat16)
    onehot[0:BLOCK, :] = own_hot
    onehot[BLOCK:, :] = own_hot

    def gather_list(h, place):
        blocks = [
            (left, me > 0), (me, None), (right, me < n - 1),
            (global_ref[0, 0], None), (global_ref[0, 1], None),
        ]
        for r in range(RAND):
            blocks.append((random_ref[0, me, h, r], None))
        for i, (block, valid) in enumerate(blocks):
            span = pl.ds(i * BLOCK, BLOCK)
            keys[place, span, 0:HD] = kvs[h][block, 0:BLOCK, :]
            values[place, span, :] = kvs[h][block, BLOCK:, :]
            doc = doc_of(block)
            if valid is not None:
                doc = jnp.where(valid, doc, -1)
            keys[place, span, HD:] = jnp.where(doc == lanes, 0.0, -1e30).astype(jnp.bfloat16)

    def attend(pair, place):
        queries = qs[pl.ds(2 * pair, 2)].reshape(2 * BLOCK, HD)
        wide = jnp.concatenate([queries, onehot[...]], axis=1)
        scores = lax.dot_general(
            wide, keys[place], (((1,), (1,)), ((), ())), preferred_element_type=jnp.float32)
        top = jnp.max(scores, axis=-1, keepdims=True)
        weights = jnp.exp2((scores - top) * FACTOR)
        sums = jnp.sum(weights, axis=-1, keepdims=True)
        product = jnp.dot(
            weights.astype(jnp.bfloat16), values[place], preferred_element_type=jnp.float32)
        result = (product / sums).astype(jnp.bfloat16)
        stream[pl.ds(2 * pair, 2)] = result.reshape(2, BLOCK, HD)

    def relay_copy(pair):
        return pltpu.make_async_remote_copy(
            src_ref=stream.at[pl.ds(2 * pair, 2)], dst_ref=arrived.at[pl.ds(2 * pair, 2)],
            send_sem=relay_send.at[pair], recv_sem=relay_recv.at[pair],
            device_id={"section": lax.rem(section + 1, section_count)}, device_id_type=MESH)

    def relay(pair):
        span = pl.ds(2 * pair, 2)

        @pl.when(section > 0)
        def _():
            relay_copy(pair).wait_recv()
            stream[span] = (
                arrived[span].astype(jnp.float32) + stream[span].astype(jnp.float32)
            ).astype(jnp.bfloat16)

        @pl.when(section < section_count - 1)
        def _():
            relay_copy(pair).start()

        wide = stream[span].astype(jnp.float32)
        squares[...] += wide[0] * wide[0] + wide[1] * wide[1]
        out_copy(2 * pair).start()
        out_copy(2 * pair + 1).start()

    def relay_behind(i):
        behind = i - LAG * section

        @pl.when(behind >= 0)
        def _():
            relay(behind)

    squares[...] = jnp.zeros_like(squares)

    def wait_inputs(u, carry):
        q_copy(u).wait()
        c_copy(u).wait()
        return carry

    def first_phase(t, carry):
        ring_step((0, 1), t)
        return carry

    lax.fori_loop(2, half + 1, first_phase, 0)
    ring_start((2, 3))
    lax.fori_loop(0, HEADS, wait_inputs, 0)
    ring_finish((0, 1))
    gather_list(0, 0)
    gather_list(1, 1)

    def second_phase(i, carry):
        ring_step((2, 3), i + 2)
        attend(i, i // 4)
        relay_behind(i)
        return carry

    lax.fori_loop(0, PAIRS // 2, second_phase, 0)
    ring_finish((2, 3))
    gather_list(2, 0)
    gather_list(3, 1)

    def third_phase(i, carry):
        attend(i, i // 4 - 2)
        relay_behind(i)
        return carry

    lax.fori_loop(PAIRS // 2, PAIRS, third_phase, 0)

    def drain(i, carry):
        @pl.when(i - LAG * section < PAIRS)
        def _():
            relay(i - LAG * section)
        return carry

    lax.fori_loop(PAIRS, PAIRS + LAG * (section_count - 1), drain, 0)

    mean = jnp.sum(squares[...], axis=-1, keepdims=True) / (HEADS * HD)
    inverse = jnp.broadcast_to(lax.rsqrt(mean + 1e-06), (BLOCK, HD))

    def term_pair(p, carry):
        parts = []
        for j in range(2):
            u = 2 * p + j
            scaled = cs[u].astype(jnp.float32) * stream[u].astype(jnp.float32) * inverse
            parts.append(jnp.sum(scaled, axis=0, keepdims=True))
        terms[p] = jnp.concatenate(parts, axis=0) / dp_count
        return carry

    lax.fori_loop(0, PAIRS, term_pair, 0)

    width = PAIRS // dp_count

    def scatter_copy(peer):
        return pltpu.make_async_remote_copy(
            src_ref=terms.at[pl.ds(peer * width, width)], dst_ref=scattered.at[dp],
            send_sem=rs_send.at[peer], recv_sem=rs_recv.at[dp],
            device_id={"dp": peer}, device_id_type=MESH)

    def scatter_arrival(peer):
        return pltpu.make_async_remote_copy(
            src_ref=terms.at[pl.ds(peer * width, width)], dst_ref=scattered.at[peer],
            send_sem=rs_send.at[peer], recv_sem=rs_recv.at[peer],
            device_id={"dp": peer}, device_id_type=MESH)

    def cross_copy(peer):
        return pltpu.make_async_remote_copy(
            src_ref=crossed.at[me], dst_ref=crossed.at[me],
            send_sem=z_send.at[peer], recv_sem=z_recv.at[me],
            device_id={"ctx": peer}, device_id_type=MESH)

    def cross_arrival(peer):
        return pltpu.make_async_remote_copy(
            src_ref=crossed.at[peer], dst_ref=crossed.at[peer],
            send_sem=z_send.at[peer], recv_sem=z_recv.at[peer],
            device_id={"ctx": peer}, device_id_type=MESH)

    def gather_copy(peer):
        return pltpu.make_async_remote_copy(
            src_ref=gathered.at[dp], dst_ref=gathered.at[dp],
            send_sem=f_send.at[peer], recv_sem=f_recv.at[dp],
            device_id={"dp": peer}, device_id_type=MESH)

    def gather_arrival(peer):
        return pltpu.make_async_remote_copy(
            src_ref=gathered.at[peer], dst_ref=gathered.at[peer],
            send_sem=f_send.at[peer], recv_sem=f_recv.at[peer],
            device_id={"dp": peer}, device_id_type=MESH)

    def each(count, own, action):
        def one(step, carry):
            action(lax.rem(own + step, count))
            return carry
        lax.fori_loop(1, count, one, 0)

    each(dp_count, dp, lambda peer: scatter_copy(peer).start())
    scattered[dp] = terms[pl.ds(dp * width, width)]
    each(dp_count, dp, lambda peer: scatter_arrival(peer).wait_recv())
    crossed[me] = jnp.sum(scattered[...], axis=0)
    each(n, me, lambda peer: cross_copy(peer).start())
    each(n, me, lambda peer: cross_arrival(peer).wait_recv())
    gathered[dp] = jnp.sum(crossed[...], axis=0)
    each(dp_count, dp, lambda peer: gather_copy(peer).start())
    each(dp_count, dp, lambda peer: gather_arrival(peer).wait_recv())
    for p in range(PAIRS):
        for j in range(2):
            u = 2 * p + j
            gain_ref[0:1, u * HD:(u + 1) * HD] = gathered[p // width, p % width, j:j + 1, :]

    each(dp_count, dp, lambda peer: scatter_copy(peer).wait_send())
    each(n, me, lambda peer: cross_copy(peer).wait_send())
    each(dp_count, dp, lambda peer: gather_copy(peer).wait_send())

    def sent(t, carry):
        for h in range(KVH):
            for d in range(2):
                ring(h, d, t, False).wait_send()
        return carry

    lax.fori_loop(1, half, sent, 0)
    for h in range(KVH):
        for d in range(2):
            ring(h, d, half, True).wait_send()

    @pl.when(section < section_count - 1)
    def _():
        def relayed(p, carry):
            relay_copy(p).wait_send()
            return carry
        lax.fori_loop(0, PAIRS, relayed, 0)

    def written(u, carry):
        out_copy(u).wait()
        return carry

    lax.fori_loop(0, HEADS, written, 0)


def per_device(queries, keys_values, random_blocks, global_blocks, doc_lengths, cotangent):
    counts = (lax.axis_size("dp"), lax.axis_size("section"), lax.axis_size("ctx"))
    dp_count, _, n = counts
    width = PAIRS // dp_count
    dma = pltpu.SemaphoreType.DMA
    small = pl.BlockSpec(memory_space=pltpu.SMEM)
    large = pl.BlockSpec(memory_space=pl.ANY)
    unit = pltpu.VMEM((HEADS, BLOCK, HD), jnp.bfloat16)
    stream, gain = pl.pallas_call(
        functools.partial(body, counts),
        out_shape=(
            jax.ShapeDtypeStruct(queries.shape, jnp.bfloat16),
            jax.ShapeDtypeStruct((1, HEADS * HD), jnp.float32),
        ),
        in_specs=[small, small, small, large, large, large],
        out_specs=(large, pl.BlockSpec(memory_space=pltpu.VMEM)),
        scratch_shapes=[pltpu.VMEM((n, 2 * BLOCK, HD), jnp.bfloat16)] * KVH + [
            unit, unit, unit, unit,
            pltpu.VMEM((2, LISTED * BLOCK, 2 * HD), jnp.bfloat16),
            pltpu.VMEM((2, LISTED * BLOCK, HD), jnp.bfloat16),
            pltpu.VMEM((2 * BLOCK, HD), jnp.bfloat16),
            pltpu.VMEM((BLOCK, HD), jnp.float32),
            pltpu.VMEM((PAIRS, 2, HD), jnp.float32),
            pltpu.VMEM((dp_count, width, 2, HD), jnp.float32),
            pltpu.VMEM((n, width, 2, HD), jnp.float32),
            pltpu.VMEM((dp_count, width, 2, HD), jnp.float32),
            dma((KVH, 2, n // 2)), dma((KVH, 2, n // 2)), dma((KVH, 2)),
            dma((HEADS,)), dma((HEADS,)), dma((HEADS,)),
            dma((PAIRS,)), dma((PAIRS,)),
            dma((dp_count,)), dma((dp_count,)), dma((n,)), dma((n,)), dma((dp_count,)), dma((dp_count,)),
        ],
        compiler_params=pltpu.CompilerParams(
            collective_id=0, has_side_effects=True, vmem_limit_bytes=48 * 1024 * 1024),
        name="relay_attention",
    )(random_blocks, global_blocks, doc_lengths, queries, keys_values, cotangent)
    return stream, gain


def solution(mesh):
    in_specs = (
        P("section", "dp", "ctx", None),
        P("section", "dp", "ctx", None),
        P("dp", None, None, None),
        P("dp", None),
        P("dp", None),
        P("section", "dp", "ctx", None),
    )
    out_specs = (P("section", "dp", "ctx", None), P("section", None))
    return jax.shard_map(
        per_device, mesh=mesh, in_specs=in_specs, out_specs=out_specs, check_vma=False
    )
```

```python
import functools
import math

import jax
import jax.numpy as jnp
from jax import lax
from jax.experimental import pallas as pl
from jax.experimental.pallas import tpu as pltpu
from jax.sharding import PartitionSpec as P

HEADS = 32
KVH = 4
HD = 128
RAND = 4
GLOBALS = 2
GROUP = 8
DOCS = 4
BLOCK = 128
LISTED = 3 + GLOBALS + RAND
PAIRS = HEADS // 2
UNIT = 4
UNITS = HEADS // UNIT
MESH = pl.DeviceIdType.MESH
FACTOR = math.log2(math.e) / math.sqrt(HD)
LAG = 1
PIECES = 2
OFFSETS = (0, 1, 3, 5)
ROWS = 2 * BLOCK // PIECES


def body(
    counts,
    random_hbm, global_hbm, length_hbm, q_hbm, kv_hbm, cot_hbm,
    stream_hbm, gain_ref,
    kv0, kv1, kv2, kv3, qs, cs, stream, arrived, keys, values, onehot, own_values, squares,
    terms, scattered, crossed, gathered,
    random_ref, global_ref, length_ref, small_sem,
    ag_send, ag_recv, kv_sem, q_sem, c_sem, out_sem,
    relay_send, relay_recv, rs_send, rs_recv, z_send, z_recv, f_send, f_recv,
):
    dp_count, section_count, n = counts
    dp, section, me = lax.axis_index("dp"), lax.axis_index("section"), lax.axis_index("ctx")
    half = n // 2
    kvs = (kv0, kv1, kv2, kv3)
    right, left = lax.rem(me + 1, n), lax.rem(me + n - 1, n)

    def local_kv(h):
        copies = []
        for part in range(2):
            column = part * KVH * HD + h * HD
            copies.append(pltpu.make_async_copy(
                kv_hbm.at[0, 0, :, pl.ds(column, HD)],
                own_values.at[h] if part else kvs[h].at[me, pl.ds(0, BLOCK)],
                kv_sem.at[h, part],
            ))
        return copies

    def q_copy(u):
        return pltpu.make_async_copy(
            q_hbm.at[0, 0, :, pl.ds(pl.multiple_of(u * HD, HD), HD)], qs.at[u], q_sem.at[u])

    def c_copy(u):
        return pltpu.make_async_copy(
            cot_hbm.at[0, 0, :, pl.ds(pl.multiple_of(u * HD, HD), HD)], cs.at[u], c_sem.at[u])

    def out_copy(u):
        return pltpu.make_async_copy(
            stream.at[u], stream_hbm.at[0, 0, :, pl.ds(pl.multiple_of(u * HD, HD), HD)], out_sem.at[u])

    def ring(h, d, t, k, landing=False):
        sign = 1 if d == 0 else -1
        origin = lax.rem(me - sign * (t if landing else t - 1) + 2 * n, n)
        place = kvs[h].at[origin, pl.ds(k * ROWS, ROWS)]
        return pltpu.make_async_remote_copy(
            src_ref=place, dst_ref=place,
            send_sem=ag_send.at[h, d, t - 1, k], recv_sem=ag_recv.at[h, d, t - 1, k],
            device_id={"ctx": right if d == 0 else left}, device_id_type=MESH)

    def order(heads, last=False):
        for h in heads:
            for k in range(PIECES):
                for d in range(2):
                    if not last or k // (PIECES // 2) == d:
                        yield h, d, k

    def ring_slot(slot):
        for h in range(KVH):
            t = slot - OFFSETS[h]
            if 1 <= t <= half:
                for _, d, k in order((h,)):
                    if t > 1:
                        ring(h, d, t - 1, k, True).wait_recv()
                    if t < half or k // (PIECES // 2) == d:
                        ring(h, d, t, k).start()

    def ring_finish(h):
        for _, d, k in order((h,), True):
            ring(h, d, half, k, True).wait_recv()

    barrier = pltpu.get_barrier_semaphore()
    for h in range(KVH):
        for copy in local_kv(h):
            copy.start()
    for target in (left, right):
        pl.semaphore_signal(barrier, inc=1, device_id={"ctx": target}, device_id_type=MESH)
    for step in (1, section_count - 1):
        pl.semaphore_signal(
            barrier, inc=1, device_id={"section": lax.rem(section + step, section_count)}, device_id_type=MESH)
    for step in range(1, dp_count):
        pl.semaphore_signal(
            barrier, inc=1, device_id={"dp": lax.rem(dp + step, dp_count)}, device_id_type=MESH)

    small = [
        pltpu.make_async_copy(source, target, small_sem.at[i])
        for i, (source, target) in enumerate(
            ((random_hbm, random_ref), (global_hbm, global_ref), (length_hbm, length_ref)))
    ]
    for copy in small:
        copy.start()

    def start_inputs(u, carry):
        q_copy(u).start()
        c_copy(u).start()
        return carry

    lax.fori_loop(0, HEADS, start_inputs, 0)
    for h in range(KVH):
        for copy in local_kv(h):
            copy.wait()
        turned = jnp.transpose(own_values[h].astype(jnp.float32))
        kvs[h][me, BLOCK:, :] = turned.astype(jnp.bfloat16)
    pl.semaphore_wait(barrier, 4 + dp_count - 1)
    ring_slot(1)

    for copy in small:
        copy.wait()
    ends = []
    total = 0
    for d in range(DOCS):
        total = total + length_ref[0, d]
        ends.append(total)
    lanes = lax.broadcasted_iota(jnp.int32, (BLOCK, HD), 1)
    rows = lax.broadcasted_iota(jnp.int32, (BLOCK, HD), 0)

    def doc_of(block):
        position = rows + block * BLOCK
        doc = jnp.zeros((BLOCK, HD), jnp.int32)
        for end in ends:
            doc = doc + jnp.where(position >= end, 1, 0)
        return doc

    own_hot = jnp.where(doc_of(me) == lanes, 1.0, 0.0).astype(jnp.bfloat16)
    for j in range(UNIT):
        onehot[j * BLOCK:(j + 1) * BLOCK, :] = own_hot

    def listed(h):
        blocks = [
            (left, me > 0), (me, None), (right, me < n - 1),
            (global_ref[0, 0], None), (global_ref[0, 1], None),
        ]
        for r in range(RAND):
            blocks.append((random_ref[0, h, r, me], None))
        return [(pl.ds(i * BLOCK, BLOCK),) + block for i, block in enumerate(blocks)]

    def mask_list(h):
        for span, block, valid in listed(h):
            doc = doc_of(block)
            if valid is not None:
                doc = jnp.where(valid, doc, -1)
            keys[h, span, HD:] = jnp.where(doc == lanes, 0.0, -1e30).astype(jnp.bfloat16)

    def gather_list(h):
        for span, block, _ in listed(h):
            keys[h, span, 0:HD] = kvs[h][block, 0:BLOCK, :]
            values[h, :, span] = kvs[h][block, BLOCK:, :]

    def attend(i):
        h = i // (UNITS // KVH)
        queries = qs[pl.ds(UNIT * i, UNIT)].reshape(UNIT * BLOCK, HD)
        wide = jnp.concatenate([queries, onehot[...]], axis=1)
        scores = lax.dot_general(
            keys[h], wide, (((1,), (1,)), ((), ())), preferred_element_type=jnp.float32)
        top = jnp.max(scores, axis=0, keepdims=True)
        weights = jnp.exp2((scores - top) * FACTOR)
        sums = jnp.sum(weights, axis=0, keepdims=True)
        product = jnp.dot(
            values[h], weights.astype(jnp.bfloat16), preferred_element_type=jnp.float32)
        result = jnp.transpose(product / sums).astype(jnp.bfloat16)
        stream[pl.ds(UNIT * i, UNIT)] = result.reshape(UNIT, BLOCK, HD)

    def relay_copy(u):
        return pltpu.make_async_remote_copy(
            src_ref=stream.at[u], dst_ref=arrived.at[u],
            send_sem=relay_send.at[u], recv_sem=relay_recv.at[u],
            device_id={"section": lax.rem(section + 1, section_count)}, device_id_type=MESH)

    def relay(i):
        for j in range(UNIT):
            u = UNIT * i + j

            @pl.when(section > 0)
            def _():
                relay_copy(u).wait_recv()
                stream[u] = (
                    arrived[u].astype(jnp.float32) + stream[u].astype(jnp.float32)
                ).astype(jnp.bfloat16)

            @pl.when(section < section_count - 1)
            def _():
                relay_copy(u).start()

            wide = stream[u].astype(jnp.float32)
            squares[...] += wide * wide
            out_copy(u).start()

    def relay_behind(i):
        behind = i - LAG * section

        @pl.when(behind >= 0)
        def _():
            relay(behind)

    squares[...] = jnp.zeros_like(squares)
    for h in range(KVH):
        mask_list(h)

    def wait_inputs(u, carry):
        q_copy(u).wait()
        c_copy(u).wait()
        return carry

    for slot in range(2, half + 1):
        ring_slot(slot)
        if slot == max(2, half - 1):
            lax.fori_loop(0, HEADS, wait_inputs, 0)

    units_of_head = UNITS // KVH

    def step(i, carry):
        for h in range(KVH):
            @pl.when(i == h * units_of_head)
            def _():
                ring_finish(h)
                gather_list(h)
        for late in range(OFFSETS[-1]):
            @pl.when(i == late)
            def _():
                ring_slot(half + 1 + late)
        attend(i)
        relay_behind(i)
        return carry

    lax.fori_loop(0, UNITS, step, 0)

    def drain(i, carry):
        @pl.when(i - LAG * section < UNITS)
        def _():
            relay(i - LAG * section)
        return carry

    lax.fori_loop(UNITS, UNITS + LAG * (section_count - 1), drain, 0)

    mean = jnp.sum(squares[...], axis=-1, keepdims=True) / (HEADS * HD)
    inverse = jnp.broadcast_to(lax.rsqrt(mean + 1e-06), (BLOCK, HD))

    def term_pair(p, carry):
        parts = []
        for j in range(2):
            u = 2 * p + j
            scaled = cs[u].astype(jnp.float32) * stream[u].astype(jnp.float32) * inverse
            parts.append(jnp.sum(scaled, axis=0, keepdims=True))
        terms[p] = jnp.concatenate(parts, axis=0) / dp_count
        return carry

    lax.fori_loop(0, PAIRS, term_pair, 0)

    width = PAIRS // dp_count

    def scatter_copy(peer):
        return pltpu.make_async_remote_copy(
            src_ref=terms.at[pl.ds(peer * width, width)], dst_ref=scattered.at[dp],
            send_sem=rs_send.at[peer], recv_sem=rs_recv.at[dp],
            device_id={"dp": peer}, device_id_type=MESH)

    def scatter_arrival(peer):
        return pltpu.make_async_remote_copy(
            src_ref=terms.at[pl.ds(peer * width, width)], dst_ref=scattered.at[peer],
            send_sem=rs_send.at[peer], recv_sem=rs_recv.at[peer],
            device_id={"dp": peer}, device_id_type=MESH)

    def cross_copy(peer):
        return pltpu.make_async_remote_copy(
            src_ref=crossed.at[me], dst_ref=crossed.at[me],
            send_sem=z_send.at[peer], recv_sem=z_recv.at[me],
            device_id={"ctx": peer}, device_id_type=MESH)

    def cross_arrival(peer):
        return pltpu.make_async_remote_copy(
            src_ref=crossed.at[peer], dst_ref=crossed.at[peer],
            send_sem=z_send.at[peer], recv_sem=z_recv.at[peer],
            device_id={"ctx": peer}, device_id_type=MESH)

    def gather_copy(peer):
        return pltpu.make_async_remote_copy(
            src_ref=gathered.at[dp], dst_ref=gathered.at[dp],
            send_sem=f_send.at[peer], recv_sem=f_recv.at[dp],
            device_id={"dp": peer}, device_id_type=MESH)

    def gather_arrival(peer):
        return pltpu.make_async_remote_copy(
            src_ref=gathered.at[peer], dst_ref=gathered.at[peer],
            send_sem=f_send.at[peer], recv_sem=f_recv.at[peer],
            device_id={"dp": peer}, device_id_type=MESH)

    def far_first(count, chip):
        return sorted(range(1, count), key=lambda step: -min(step // chip, (count - step) // chip))

    def each(count, chip, own, action):
        for step in far_first(count, chip):
            action(lax.rem(own + step, count))

    each(dp_count, 2, dp, lambda peer: scatter_copy(peer).start())
    scattered[dp] = terms[pl.ds(dp * width, width)]

    def written(u, carry):
        out_copy(u).wait()
        return carry

    lax.fori_loop(0, HEADS, written, 0)
    each(dp_count, 2, dp, lambda peer: scatter_arrival(peer).wait_recv())
    crossed[me] = jnp.sum(scattered[...], axis=0)
    each(n, 1, me, lambda peer: cross_copy(peer).start())

    def sent(t, carry):
        for h, d, k in order(range(KVH)):
            ring(h, d, t, k).wait_send()
        return carry

    lax.fori_loop(1, half, sent, 0)
    for h, d, k in order(range(KVH), True):
        ring(h, d, half, k).wait_send()

    @pl.when(section < section_count - 1)
    def _():
        def relayed(u, carry):
            relay_copy(u).wait_send()
            return carry
        lax.fori_loop(0, HEADS, relayed, 0)

    each(dp_count, 2, dp, lambda peer: scatter_copy(peer).wait_send())
    each(n, 1, me, lambda peer: cross_arrival(peer).wait_recv())
    gathered[dp] = jnp.sum(crossed[...], axis=0)
    each(dp_count, 2, dp, lambda peer: gather_copy(peer).start())
    each(n, 1, me, lambda peer: cross_copy(peer).wait_send())
    each(dp_count, 2, dp, lambda peer: gather_arrival(peer).wait_recv())
    for p in range(PAIRS):
        for j in range(2):
            u = 2 * p + j
            gain_ref[0:1, u * HD:(u + 1) * HD] = gathered[p // width, p % width, j:j + 1, :]
    each(dp_count, 2, dp, lambda peer: gather_copy(peer).wait_send())


def per_device(queries, keys_values, random_blocks, global_blocks, doc_lengths, cotangent):
    counts = (lax.axis_size("dp"), lax.axis_size("section"), lax.axis_size("ctx"))
    dp_count, _, n = counts
    width = PAIRS // dp_count
    dma = pltpu.SemaphoreType.DMA
    held = pl.BlockSpec(memory_space=pltpu.HBM)
    large = pl.BlockSpec(memory_space=pl.ANY)
    unit = pltpu.VMEM((HEADS, BLOCK, HD), jnp.bfloat16)
    stream, gain = pl.pallas_call(
        functools.partial(body, counts),
        out_shape=(
            jax.ShapeDtypeStruct(queries.shape, jnp.bfloat16),
            jax.ShapeDtypeStruct((1, HEADS * HD), jnp.float32),
        ),
        in_specs=[held] * 6,
        out_specs=(large, pl.BlockSpec(memory_space=pltpu.VMEM)),
        scratch_shapes=[pltpu.VMEM((n, 2 * BLOCK, HD), jnp.bfloat16)] * KVH + [
            unit, unit, unit, unit,
            pltpu.VMEM((KVH, LISTED * BLOCK, 2 * HD), jnp.bfloat16),
            pltpu.VMEM((KVH, HD, LISTED * BLOCK), jnp.bfloat16),
            pltpu.VMEM((UNIT * BLOCK, HD), jnp.bfloat16),
            pltpu.VMEM((KVH, BLOCK, HD), jnp.bfloat16),
            pltpu.VMEM((BLOCK, HD), jnp.float32),
            pltpu.VMEM((PAIRS, 2, HD), jnp.float32),
            pltpu.VMEM((dp_count, width, 2, HD), jnp.float32),
            pltpu.VMEM((n, width, 2, HD), jnp.float32),
            pltpu.VMEM((dp_count, width, 2, HD), jnp.float32),
            pltpu.SMEM((1, KVH, RAND, n), jnp.int32),
            pltpu.SMEM((1, GLOBALS), jnp.int32),
            pltpu.SMEM((1, DOCS), jnp.int32),
            dma((3,)),
            dma((KVH, 2, n // 2, PIECES)), dma((KVH, 2, n // 2, PIECES)), dma((KVH, 2)),
            dma((HEADS,)), dma((HEADS,)), dma((HEADS,)),
            dma((HEADS,)), dma((HEADS,)),
            dma((dp_count,)), dma((dp_count,)), dma((n,)), dma((n,)), dma((dp_count,)), dma((dp_count,)),
        ],
        compiler_params=pltpu.CompilerParams(
            collective_id=0, has_side_effects=True, vmem_limit_bytes=67043328),
        name="relay_attention",
    )(jnp.transpose(random_blocks, (0, 2, 3, 1)), global_blocks, doc_lengths, queries, keys_values, cotangent)
    return stream, gain


def solution(mesh):
    in_specs = (
        P("section", "dp", "ctx", None),
        P("section", "dp", "ctx", None),
        P("dp", None, None, None),
        P("dp", None),
        P("dp", None),
        P("section", "dp", "ctx", None),
    )
    out_specs = (P("section", "dp", "ctx", None), P("section", None))
    return jax.shard_map(
        per_device, mesh=mesh, in_specs=in_specs, out_specs=out_specs, check_vma=False
    )
```

```python
import functools
import math

import jax
import jax.numpy as jnp
from jax import lax
from jax.experimental import pallas as pl
from jax.experimental.pallas import tpu as pltpu
from jax.sharding import PartitionSpec as P

HEADS = 32
KVH = 4
HD = 128
RAND = 4
GLOBALS = 2
GROUP = 8
DOCS = 4
BLOCK = 128
LISTED = 3 + GLOBALS + RAND
PAIRS = HEADS // 2
UNIT = 4
UNITS = HEADS // UNIT
MESH = pl.DeviceIdType.MESH
FACTOR = math.log2(math.e) / math.sqrt(HD)
LAG = 1
PIECES = 2
OFFSETS = (0, 1, 3, 5)
ROWS = 2 * BLOCK // PIECES


def body(
    counts,
    random_hbm, global_hbm, length_hbm, q_hbm, kv_hbm, cot_hbm,
    stream_hbm, gain_ref,
    kv0, kv1, kv2, kv3, qs, cs, stream, arrived, keys, values, onehot, own_values, squares,
    terms, scattered, crossed, gathered,
    random_ref, global_ref, length_ref, small_sem,
    ag_send, ag_recv, kv_sem, q_sem, c_sem, out_sem,
    relay_send, relay_recv, rs_send, rs_recv, z_send, z_recv, f_send, f_recv,
):
    dp_count, section_count, n = counts
    dp, section, me = lax.axis_index("dp"), lax.axis_index("section"), lax.axis_index("ctx")
    half = n // 2
    kvs = (kv0, kv1, kv2, kv3)
    right, left = lax.rem(me + 1, n), lax.rem(me + n - 1, n)

    def local_kv(h):
        copies = []
        for part in range(2):
            column = part * KVH * HD + h * HD
            copies.append(pltpu.make_async_copy(
                kv_hbm.at[0, 0, :, pl.ds(column, HD)],
                own_values.at[h] if part else kvs[h].at[me, pl.ds(0, BLOCK)],
                kv_sem.at[h, part],
            ))
        return copies

    def q_copy(u):
        return pltpu.make_async_copy(
            q_hbm.at[0, 0, :, pl.ds(pl.multiple_of(u * HD, HD), HD)], qs.at[u], q_sem.at[u])

    def c_copy(u):
        return pltpu.make_async_copy(
            cot_hbm.at[0, 0, :, pl.ds(pl.multiple_of(u * HD, HD), HD)], cs.at[u], c_sem.at[u])

    def out_copy(u):
        return pltpu.make_async_copy(
            stream.at[u], stream_hbm.at[0, 0, :, pl.ds(pl.multiple_of(u * HD, HD), HD)], out_sem.at[u])

    def ring(h, d, t, k, landing=False):
        sign = 1 if d == 0 else -1
        origin = lax.rem(me - sign * (t if landing else t - 1) + 2 * n, n)
        place = kvs[h].at[origin, pl.ds(k * ROWS, ROWS)]
        return pltpu.make_async_remote_copy(
            src_ref=place, dst_ref=place,
            send_sem=ag_send.at[h, d, t - 1, k], recv_sem=ag_recv.at[h, d, t - 1, k],
            device_id={"ctx": right if d == 0 else left}, device_id_type=MESH)

    def order(heads, last=False):
        for h in heads:
            for k in range(PIECES):
                for d in range(2):
                    if not last or k // (PIECES // 2) == d:
                        yield h, d, k

    def ring_slot(slot):
        for h in range(KVH):
            t = slot - OFFSETS[h]
            if 1 <= t <= half:
                for _, d, k in order((h,)):
                    if t > 1:
                        ring(h, d, t - 1, k, True).wait_recv()
                    if t < half or k // (PIECES // 2) == d:
                        ring(h, d, t, k).start()

    def ring_finish(h):
        for _, d, k in order((h,), True):
            ring(h, d, half, k, True).wait_recv()

    barrier = pltpu.get_barrier_semaphore()
    for h in range(KVH):
        for copy in local_kv(h):
            copy.start()
    for target in (left, right):
        pl.semaphore_signal(barrier, inc=1, device_id={"ctx": target}, device_id_type=MESH)
    for step in (1, section_count - 1):
        pl.semaphore_signal(
            barrier, inc=1, device_id={"section": lax.rem(section + step, section_count)}, device_id_type=MESH)
    for step in range(1, dp_count):
        pl.semaphore_signal(
            barrier, inc=1, device_id={"dp": lax.rem(dp + step, dp_count)}, device_id_type=MESH)

    small = [
        pltpu.make_async_copy(source, target, small_sem.at[i])
        for i, (source, target) in enumerate(
            ((random_hbm, random_ref), (global_hbm, global_ref), (length_hbm, length_ref)))
    ]
    for copy in small:
        copy.start()

    def start_inputs(u, carry):
        q_copy(u).start()
        c_copy(u).start()
        return carry

    lax.fori_loop(0, HEADS, start_inputs, 0)
    for h in range(KVH):
        for copy in local_kv(h):
            copy.wait()
        turned = jnp.transpose(own_values[h].astype(jnp.float32))
        kvs[h][me, BLOCK:, :] = turned.astype(jnp.bfloat16)
    pl.semaphore_wait(barrier, 4 + dp_count - 1)
    ring_slot(1)

    for copy in small:
        copy.wait()
    ends = []
    total = 0
    for d in range(DOCS):
        total = total + length_ref[0, d]
        ends.append(total)
    lanes = lax.broadcasted_iota(jnp.int32, (BLOCK, HD), 1)
    rows = lax.broadcasted_iota(jnp.int32, (BLOCK, HD), 0)

    def doc_of(block):
        position = rows + block * BLOCK
        doc = jnp.zeros((BLOCK, HD), jnp.int32)
        for end in ends:
            doc = doc + jnp.where(position >= end, 1, 0)
        return doc

    own_hot = jnp.where(doc_of(me) == lanes, 1.0, 0.0).astype(jnp.bfloat16)
    for j in range(UNIT):
        onehot[j * BLOCK:(j + 1) * BLOCK, :] = own_hot

    def listed(h):
        blocks = [
            (left, me > 0), (me, None), (right, me < n - 1),
            (global_ref[0, 0], None), (global_ref[0, 1], None),
        ]
        for r in range(RAND):
            blocks.append((random_ref[0, h, r, me], None))
        return [(pl.ds(i * BLOCK, BLOCK),) + block for i, block in enumerate(blocks)]

    def mask_list(h):
        for span, block, valid in listed(h):
            doc = doc_of(block)
            if valid is not None:
                doc = jnp.where(valid, doc, -1)
            keys[h, span, HD:] = jnp.where(doc == lanes, 0.0, -1e30).astype(jnp.bfloat16)

    def gather_list(h):
        for span, block, _ in listed(h):
            keys[h, span, 0:HD] = kvs[h][block, 0:BLOCK, :]
            values[h, :, span] = kvs[h][block, BLOCK:, :]

    def attend(i):
        h = i // (UNITS // KVH)
        queries = qs[pl.ds(UNIT * i, UNIT)].reshape(UNIT * BLOCK, HD)
        wide = jnp.concatenate([queries, onehot[...]], axis=1)
        scores = lax.dot_general(
            keys[h], wide, (((1,), (1,)), ((), ())), preferred_element_type=jnp.float32)
        top = jnp.max(scores, axis=0, keepdims=True)
        weights = jnp.exp2((scores - top) * FACTOR)
        sums = jnp.sum(weights, axis=0, keepdims=True)
        product = jnp.dot(
            values[h], weights.astype(jnp.bfloat16), preferred_element_type=jnp.float32)
        result = jnp.transpose(product / sums).astype(jnp.bfloat16)
        stream[pl.ds(UNIT * i, UNIT)] = result.reshape(UNIT, BLOCK, HD)

    def relay_copy(u):
        return pltpu.make_async_remote_copy(
            src_ref=stream.at[u], dst_ref=arrived.at[u],
            send_sem=relay_send.at[u], recv_sem=relay_recv.at[u],
            device_id={"section": lax.rem(section + 1, section_count)}, device_id_type=MESH)

    def relay(i):
        for j in range(UNIT):
            u = UNIT * i + j

            @pl.when(section > 0)
            def _():
                relay_copy(u).wait_recv()
                stream[u] = (
                    arrived[u].astype(jnp.float32) + stream[u].astype(jnp.float32)
                ).astype(jnp.bfloat16)

            @pl.when(section < section_count - 1)
            def _():
                relay_copy(u).start()

            wide = stream[u].astype(jnp.float32)
            squares[...] += wide * wide
            out_copy(u).start()

    def relay_behind(i):
        behind = i - LAG * section

        @pl.when(behind >= 0)
        def _():
            relay(behind)

    squares[...] = jnp.zeros_like(squares)
    for h in range(KVH):
        mask_list(h)

    def wait_inputs(u, carry):
        q_copy(u).wait()
        c_copy(u).wait()
        return carry

    for slot in range(2, half + 1):
        ring_slot(slot)
        if slot == max(2, half - 1):
            lax.fori_loop(0, HEADS, wait_inputs, 0)

    units_of_head = UNITS // KVH

    def step(i, carry):
        for h in range(KVH):
            @pl.when(i == h * units_of_head)
            def _():
                ring_finish(h)
                gather_list(h)
        for late in range(OFFSETS[-1]):
            @pl.when(i == late)
            def _():
                ring_slot(half + 1 + late)
        attend(i)
        relay_behind(i)
        return carry

    lax.fori_loop(0, UNITS, step, 0)

    def drain(i, carry):
        @pl.when(i - LAG * section < UNITS)
        def _():
            relay(i - LAG * section)
        return carry

    lax.fori_loop(UNITS, UNITS + LAG * (section_count - 1), drain, 0)

    mean = jnp.sum(squares[...], axis=-1, keepdims=True) / (HEADS * HD)
    inverse = jnp.broadcast_to(lax.rsqrt(mean + 1e-06), (BLOCK, HD))

    width = PAIRS // dp_count

    def scatter_copy(peer):
        return pltpu.make_async_remote_copy(
            src_ref=terms.at[pl.ds(peer * width, width)], dst_ref=scattered.at[dp],
            send_sem=rs_send.at[peer], recv_sem=rs_recv.at[dp],
            device_id={"dp": peer}, device_id_type=MESH)

    def scatter_arrival(peer):
        return pltpu.make_async_remote_copy(
            src_ref=terms.at[pl.ds(peer * width, width)], dst_ref=scattered.at[peer],
            send_sem=rs_send.at[peer], recv_sem=rs_recv.at[peer],
            device_id={"dp": peer}, device_id_type=MESH)

    def cross_copy(peer):
        return pltpu.make_async_remote_copy(
            src_ref=crossed.at[me], dst_ref=crossed.at[me],
            send_sem=z_send.at[peer], recv_sem=z_recv.at[me],
            device_id={"ctx": peer}, device_id_type=MESH)

    def cross_arrival(peer):
        return pltpu.make_async_remote_copy(
            src_ref=crossed.at[peer], dst_ref=crossed.at[peer],
            send_sem=z_send.at[peer], recv_sem=z_recv.at[peer],
            device_id={"ctx": peer}, device_id_type=MESH)

    def gather_copy(peer):
        return pltpu.make_async_remote_copy(
            src_ref=gathered.at[dp], dst_ref=gathered.at[dp],
            send_sem=f_send.at[peer], recv_sem=f_recv.at[dp],
            device_id={"dp": peer}, device_id_type=MESH)

    def gather_arrival(peer):
        return pltpu.make_async_remote_copy(
            src_ref=gathered.at[peer], dst_ref=gathered.at[peer],
            send_sem=f_send.at[peer], recv_sem=f_recv.at[peer],
            device_id={"dp": peer}, device_id_type=MESH)

    def far_first(count, chip):
        return sorted(range(1, count), key=lambda step: -min(step // chip, (count - step) // chip))

    def each(count, chip, own, action):
        for step in far_first(count, chip):
            action(lax.rem(own + step, count))

    def peer_at(i):
        middle = dp_count // 2
        step = jnp.where(lax.rem(i, 2) == 1, middle - (i + 1) // 2, middle + i // 2)
        return lax.rem(dp + step, dp_count)

    def term_piece(i, carry):
        first = peer_at(i) * width
        for w in range(width):
            p = first + w
            parts = []
            for j in range(2):
                u = 2 * p + j
                scaled = cs[u].astype(jnp.float32) * stream[u].astype(jnp.float32) * inverse
                parts.append(jnp.sum(scaled, axis=0, keepdims=True))
            terms[p] = jnp.concatenate(parts, axis=0) / dp_count

        @pl.when(i > 0)
        def _():
            scatter_copy(peer_at(i - 1)).start()
        return carry

    lax.fori_loop(0, dp_count, term_piece, 0)
    scattered[dp] = terms[pl.ds(dp * width, width)]

    def written(u, carry):
        out_copy(u).wait()
        return carry

    lax.fori_loop(0, HEADS, written, 0)
    each(dp_count, 2, dp, lambda peer: scatter_arrival(peer).wait_recv())
    crossed[me] = jnp.sum(scattered[...], axis=0)
    each(n, 1, me, lambda peer: cross_copy(peer).start())

    def sent(t, carry):
        for h, d, k in order(range(KVH)):
            ring(h, d, t, k).wait_send()
        return carry

    lax.fori_loop(1, half, sent, 0)
    for h, d, k in order(range(KVH), True):
        ring(h, d, half, k).wait_send()

    @pl.when(section < section_count - 1)
    def _():
        def relayed(u, carry):
            relay_copy(u).wait_send()
            return carry
        lax.fori_loop(0, HEADS, relayed, 0)

    each(dp_count, 2, dp, lambda peer: scatter_copy(peer).wait_send())
    each(n, 1, me, lambda peer: cross_arrival(peer).wait_recv())
    gathered[dp] = jnp.sum(crossed[...], axis=0)
    each(dp_count, 2, dp, lambda peer: gather_copy(peer).start())
    each(n, 1, me, lambda peer: cross_copy(peer).wait_send())
    each(dp_count, 2, dp, lambda peer: gather_arrival(peer).wait_recv())
    for p in range(PAIRS):
        for j in range(2):
            u = 2 * p + j
            gain_ref[0:1, u * HD:(u + 1) * HD] = gathered[p // width, p % width, j:j + 1, :]
    each(dp_count, 2, dp, lambda peer: gather_copy(peer).wait_send())


def per_device(queries, keys_values, random_blocks, global_blocks, doc_lengths, cotangent):
    counts = (lax.axis_size("dp"), lax.axis_size("section"), lax.axis_size("ctx"))
    dp_count, _, n = counts
    width = PAIRS // dp_count
    dma = pltpu.SemaphoreType.DMA
    held = pl.BlockSpec(memory_space=pltpu.HBM)
    large = pl.BlockSpec(memory_space=pl.ANY)
    unit = pltpu.VMEM((HEADS, BLOCK, HD), jnp.bfloat16)
    stream, gain = pl.pallas_call(
        functools.partial(body, counts),
        out_shape=(
            jax.ShapeDtypeStruct(queries.shape, jnp.bfloat16),
            jax.ShapeDtypeStruct((1, HEADS * HD), jnp.float32),
        ),
        in_specs=[held] * 6,
        out_specs=(large, pl.BlockSpec(memory_space=pltpu.VMEM)),
        scratch_shapes=[pltpu.VMEM((n, 2 * BLOCK, HD), jnp.bfloat16)] * KVH + [
            unit, unit, unit, unit,
            pltpu.VMEM((KVH, LISTED * BLOCK, 2 * HD), jnp.bfloat16),
            pltpu.VMEM((KVH, HD, LISTED * BLOCK), jnp.bfloat16),
            pltpu.VMEM((UNIT * BLOCK, HD), jnp.bfloat16),
            pltpu.VMEM((KVH, BLOCK, HD), jnp.bfloat16),
            pltpu.VMEM((BLOCK, HD), jnp.float32),
            pltpu.VMEM((PAIRS, 2, HD), jnp.float32),
            pltpu.VMEM((dp_count, width, 2, HD), jnp.float32),
            pltpu.VMEM((n, width, 2, HD), jnp.float32),
            pltpu.VMEM((dp_count, width, 2, HD), jnp.float32),
            pltpu.SMEM((1, KVH, RAND, n), jnp.int32),
            pltpu.SMEM((1, GLOBALS), jnp.int32),
            pltpu.SMEM((1, DOCS), jnp.int32),
            dma((3,)),
            dma((KVH, 2, n // 2, PIECES)), dma((KVH, 2, n // 2, PIECES)), dma((KVH, 2)),
            dma((HEADS,)), dma((HEADS,)), dma((HEADS,)),
            dma((HEADS,)), dma((HEADS,)),
            dma((dp_count,)), dma((dp_count,)), dma((n,)), dma((n,)), dma((dp_count,)), dma((dp_count,)),
        ],
        compiler_params=pltpu.CompilerParams(
            collective_id=0, has_side_effects=True, vmem_limit_bytes=67043328),
        name="relay_attention",
    )(jnp.transpose(random_blocks, (0, 2, 3, 1)), global_blocks, doc_lengths, queries, keys_values, cotangent)
    return stream, gain


def solution(mesh):
    in_specs = (
        P("section", "dp", "ctx", None),
        P("section", "dp", "ctx", None),
        P("dp", None, None, None),
        P("dp", None),
        P("dp", None),
        P("section", "dp", "ctx", None),
    )
    out_specs = (P("section", "dp", "ctx", None), P("section", None))
    return jax.shard_map(
        per_device, mesh=mesh, in_specs=in_specs, out_specs=out_specs, check_vma=False
    )
```
